32 devices in a mesh: role: 4 (over y, core), shard: 8 (over z, x).
Axes of the slice: x: 2, y: 2, z: 4, core: 2. Of those that a mesh axis runs over, the one named last changes fastest.
Arguments:
- gradient: bfloat16 [2560, 2560], P('shard', 'role'), may hold values from -1200 to 1200
- left_old: float32 [2560, 2560], P('shard', 'role'), may hold values from -1 to 10, as said below
- right_old: float32 [2560, 2560], P('shard', 'role'), may hold values from -1 to 10, as said below
- basis_old: bfloat16 [2560, 512], P('shard', 'role'), may hold values from -1 to 1
Outputs:
- left_stat: float32 [2560, 2560], P('shard', 'role')
- right_stat: float32 [2560, 2560], P('shard', 'role')
- left_basis: float32 [2560, 512], P('shard', 'role')
The draws below stay inside these ranges and needn't reach their ends.
Inputs may be any that keep to these rules, and one draw needn't show every extreme that they name: `left_old`: symmetric and positive definite. `right_old`: symmetric and positive definite.
All inputs are finite; a program needn't handle non-finite values.
Results may differ from the reference program's by a relative error of at most 0.0003.
Values may be sent and summed in bfloat16 or wider, within the bound.
No kernel may reach another device: no remote copies, remote signals or barrier semaphores. Data moves between devices by JAX's collectives and lax.ppermute only.
A program may use at most 64 MiB of HBM per device.

```python
import jax
import jax.numpy as jnp
from jax import lax

BLK = 2560
VEC = 512


def scale_profile(key, length):
    ramp = jnp.exp(jnp.log(10.0) * jnp.arange(length, dtype=jnp.float32) / (length - 1))
    jitter = jax.random.uniform(key, (length,), jnp.float32, 0.8, 1.25)
    return ramp * jitter


def draw_gradient(key, part):
    base = jax.random.fold_in(key, 5)
    key_rows = jax.random.fold_in(base, 1)
    key_cols = jax.random.fold_in(base, 2)
    key_body = jax.random.fold_in(base, 3)
    row_scale = scale_profile(key_rows, BLK)
    col_scale = scale_profile(key_cols, BLK)
    rough = jax.random.normal(key_body, (BLK, BLK), jnp.float32)
    values = row_scale[:, None] * col_scale[None, :] * rough
    return jnp.clip(values, -1200.0, 1200.0).astype(jnp.bfloat16)


def symmetric_draw(key):
    key_diag = jax.random.fold_in(key, 1)
    key_noise = jax.random.fold_in(key, 2)
    diagonal = jnp.exp(jax.random.uniform(key_diag, (BLK,), jnp.float32, jnp.log(4.0), jnp.log(9.0)))
    noise = jax.random.normal(key_noise, (BLK, BLK), jnp.float32)
    noise = (noise + noise.T) * (1.5 / jnp.sqrt(2.0 * BLK))
    return jnp.clip(noise, -1.0, 1.0) + jnp.diag(diagonal)


def draw_left_old(key, part):
    return symmetric_draw(jax.random.fold_in(key, 21))


def draw_right_old(key, part):
    return symmetric_draw(jax.random.fold_in(key, 22))


def draw_basis_old(key, part):
    key_basis = jax.random.fold_in(key, 31)
    source = jax.random.normal(key_basis, (BLK, VEC), jnp.float32)
    orthonormal = jnp.linalg.qr(source)[0]
    return jnp.clip(orthonormal, -1.0, 1.0).astype(jnp.bfloat16)


def setup_inputs(seed: int = 0) -> dict:
    keys = jax.random.split(jax.random.key(seed), 5)
    return {
        "gradient": draw_gradient(jax.random.fold_in(keys[4], 71), 0),
        "left_old": draw_left_old(jax.random.fold_in(keys[4], 71), 0),
        "right_old": draw_right_old(jax.random.fold_in(keys[4], 71), 0),
        "basis_old": draw_basis_old(jax.random.fold_in(keys[4], 71), 0),
    }


smoothing = 0.95
clip_ratio = 4.0
epsilon_value = 1e-06

def reference(gradient, left_old, right_old, basis_old):
    gradient_wide = gradient.astype(jnp.float32)
    squares = jnp.sum(gradient_wide * gradient_wide)
    factor = jnp.minimum(1.0, clip_ratio * jnp.sqrt(jnp.float32(BLK)) / jnp.sqrt(squares + epsilon_value))
    squared = factor * factor
    left_gram = jnp.dot(gradient.astype(jnp.float32), gradient.T.astype(jnp.float32), preferred_element_type=jnp.float32)
    right_gram = jnp.dot(gradient.T.astype(jnp.float32), gradient.astype(jnp.float32), preferred_element_type=jnp.float32)
    left_stat = smoothing * left_old + (1.0 - smoothing) * squared * left_gram
    right_stat = smoothing * right_old + (1.0 - smoothing) * squared * right_gram
    power = jnp.dot(left_stat, basis_old.astype(jnp.float32), precision=lax.Precision.HIGHEST)
    gram_full = jnp.dot(power.T, power, precision=lax.Precision.HIGHEST)
    factor_lower = jnp.linalg.cholesky(gram_full)
    left_basis = jax.scipy.linalg.solve_triangular(factor_lower, power.T, lower=True).T
    return (left_stat, right_stat, left_basis)
```

```python
import jax
import jax.numpy as jnp
from jax import lax
from jax.experimental import pallas as pl
from jax.experimental.pallas import tpu as pltpu
from jax.sharding import PartitionSpec as P

smoothing = 0.95
clip_ratio = 4.0
epsilon_value = 1e-06


HI = lax.Precision.HIGHEST
BLOCK, PANEL = 128, 8

def factor_block(t_ref):
    w = PANEL
    sub = lax.broadcasted_iota(jnp.int32, (w, 128), 0)
    full = lambda v: jnp.broadcast_to(v, (w, 128))
    for p in range(BLOCK // w):
        c0 = p * w
        left, right = t_ref[c0:c0 + w, 0:128], t_ref[c0:c0 + w, 128:256]
        cols = [full(left[:, c0 + k:c0 + k + 1]) for k in range(w)]
        e = {(i, k): full(cols[k][i:i + 1, :]) for i in range(w) for k in range(i + 1)}
        l, inv, rs = {}, [], []
        for j in range(w):
            r = 1.0 / e[j, j]
            inv.append(r); rs.append(lax.rsqrt(e[j, j]))
            for i in range(j + 1, w):
                l[i, j] = e[i, j] * r
            for i in range(j + 1, w):
                for k in range(j + 1, i + 1):
                    e[i, k] = e[i, k] - l[i, j] * e[k, j]
        li = {}
        for k in range(w):
            for i in range(k + 1, w):
                acc = l[i, k]
                for m in range(k + 1, i):
                    acc = acc + l[i, m] * li[m, k]
                li[i, k] = -acc
        def pick(vals):
            out = jnp.zeros((w, 128), jnp.float32)
            for i, v in vals.items():
                out = jnp.where(sub == i, v, out)
            return out
        zl, zr = left, right
        for k in range(w - 1):
            coef = pick({i: li[i, k] for i in range(k + 1, w)})
            zl = zl + coef * full(left[k:k + 1, :])
            zr = zr + coef * full(right[k:k + 1, :])
        dinv = pick(dict(enumerate(inv)))
        ul, ur = dinv * zl, dinv * zr
        vl, vr = ul, ur
        for k in range(1, w):
            coef = pick({i: li[k, i] for i in range(k)})
            vl = vl + coef * full(ul[k:k + 1, :])
            vr = vr + coef * full(ur[k:k + 1, :])
        vlb = [full(vl[k:k + 1, :]) for k in range(w)]
        vrb = [full(vr[k:k + 1, :]) for k in range(w)]
        for q in range(p + 1, BLOCK // w):
            rows = slice(q * w, q * w + w)
            al, ar = t_ref[rows, 0:128], t_ref[rows, 128:256]
            nl, nr = al, ar
            for k in range(w):
                a = full(al[:, c0 + k:c0 + k + 1])
                nl = nl - a * vlb[k]
                nr = nr - a * vrb[k]
            t_ref[rows, 0:128] = nl
            t_ref[rows, 128:256] = nr
        scale = pick(dict(enumerate(rs)))
        t_ref[c0:c0 + w, 0:128] = scale * zl
        t_ref[c0:c0 + w, 128:256] = scale * zr

def chol_kernel(g_ref, o_ref, m_ref, t_ref):
    n = g_ref.shape[0]
    nb = n // BLOCK
    m_ref[:, :n] = g_ref[...]
    m_ref[:, n:] = (lax.broadcasted_iota(jnp.int32, (n, n), 0) == lax.broadcasted_iota(jnp.int32, (n, n), 1)).astype(jnp.float32)
    eye = (lax.broadcasted_iota(jnp.int32, (BLOCK, BLOCK), 0) == lax.broadcasted_iota(jnp.int32, (BLOCK, BLOCK), 1)).astype(jnp.float32)
    @pl.loop(0, nb)
    def _(b):
        r0 = pl.multiple_of(b * BLOCK, BLOCK)
        t_ref[:, 0:BLOCK] = m_ref[pl.ds(r0, BLOCK), pl.ds(r0, BLOCK)]
        t_ref[:, BLOCK:] = eye
        factor_block(t_ref)
        for c in range(nb):
            @pl.when(b == c)
            def _():
                lo, hi = c * BLOCK, n + (c + 1) * BLOCK
                rows = jnp.dot(t_ref[:, BLOCK:], m_ref[lo:lo + BLOCK, lo:hi], precision=HI, preferred_element_type=jnp.float32)
                m_ref[lo:lo + BLOCK, lo:hi] = rows
                if c + 1 < nb:
                    m_ref[lo + BLOCK:, lo + BLOCK:hi] -= lax.dot_general(rows[:, BLOCK:n - lo], rows[:, BLOCK:], (((0,), (0,)), ((), ())), precision=HI, preferred_element_type=jnp.float32)
    o_ref[...] = m_ref[:, n:]

def inverse_factor(gram):
    n = gram.shape[0]
    return pl.pallas_call(chol_kernel, out_shape=jax.ShapeDtypeStruct((n, n), jnp.float32),
        scratch_shapes=[pltpu.VMEM((n, 2 * n), jnp.float32), pltpu.VMEM((BLOCK, 2 * BLOCK), jnp.float32)])(gram)


def lower_gram(power_row, role_count, role_at):
    order_size = power_row.shape[1]
    tile_size = order_size // (2 * role_count)
    second_row = 2 * role_count - 1 - role_at

    def strip(tile_row):
        chosen = lax.dynamic_slice_in_dim(power_row, tile_row * tile_size, tile_size, 1)
        return lax.dot_general(
            chosen,
            power_row,
            (((0,), (0,)), ((), ())),
            precision=lax.Precision.HIGHEST,
            preferred_element_type=jnp.float32,
        )

    strip_first = strip(role_at)
    strip_second = strip(second_row)
    split_at = (role_at + 1) * tile_size
    packed_width = order_size + tile_size
    first_ext = jnp.concatenate(
        [strip_first, jnp.zeros((tile_size, tile_size), jnp.float32)], axis=1
    )
    padded_second = jnp.concatenate(
        [jnp.zeros((tile_size, order_size), jnp.float32), strip_second], axis=1
    )
    second_ext = lax.dynamic_slice_in_dim(padded_second, order_size - split_at, packed_width, 1)
    columns = lax.broadcasted_iota(jnp.int32, (tile_size, packed_width), 1)
    packed = jnp.where(columns < split_at, first_ext, second_ext)
    tile_sums = lax.psum(packed, "shard")
    strips = lax.all_gather(tile_sums, "role", axis=0, tiled=True)
    lower_part = jnp.zeros((order_size, order_size), jnp.float32)
    for member in range(role_count):
        packed_row = strips[member * tile_size : (member + 1) * tile_size]
        head = (member + 1) * tile_size
        other = 2 * role_count - 1 - member
        tail = (2 * role_count - member) * tile_size
        lower_part = lower_part.at[member * tile_size : head, :head].set(packed_row[:, :head])
        lower_part = lower_part.at[other * tile_size : (other + 1) * tile_size, :tail].set(
            packed_row[:, head : head + tail]
        )
    return jnp.tril(lower_part) + jnp.transpose(jnp.tril(lower_part, -1))


def on_device(gradient, left_old, right_old, basis_old):
    row_count, col_count = gradient.shape
    vec_count = basis_old.shape[1]
    order_size = row_count * lax.axis_size("shard")
    role_count = lax.axis_size("role")
    role_at = lax.axis_index("role")
    col_start = role_at * col_count
    vec_start = role_at * vec_count
    gradient_wide = gradient.astype(jnp.float32)
    squares = lax.psum(jnp.sum(gradient_wide * gradient_wide), ("role", "shard"))
    factor = jnp.minimum(
        1.0, clip_ratio * jnp.sqrt(jnp.float32(order_size)) / jnp.sqrt(squares + epsilon_value)
    )
    squared = factor * factor
    grad_row = lax.all_gather(gradient, "role", axis=1, tiled=True)
    left_part = lax.dot_general(
        gradient,
        lax.all_gather(gradient, "shard", axis=0, tiled=True),
        (((1,), (1,)), ((), ())),
        preferred_element_type=jnp.float32,
    )
    right_share = lax.psum_scatter(
        lax.dot_general(
            grad_row, gradient, (((0,), (0,)), ((), ())), preferred_element_type=jnp.float32
        ),
        "shard",
        scatter_dimension=0,
        tiled=True,
    )
    placed = lax.dynamic_update_slice_in_dim(
        jnp.zeros((row_count, order_size), jnp.float32), left_old, col_start, 1
    )
    left_row = lax.psum((1.0 - smoothing) * squared * left_part + smoothing * placed, "role")
    left_stat = lax.dynamic_slice_in_dim(left_row, col_start, col_count, 1)
    right_stat = smoothing * right_old + (1.0 - smoothing) * squared * right_share
    power_block = jnp.dot(
        left_row,
        lax.all_gather(basis_old, "shard", axis=0, tiled=True).astype(jnp.float32),
        precision=lax.Precision.HIGHEST,
    )
    power_row = lax.all_gather(power_block, "role", axis=1, tiled=True)
    gram_full = lower_gram(power_row, role_count, role_at)
    inverse = inverse_factor(gram_full)
    mine = lax.dynamic_slice_in_dim(inverse, vec_start, vec_count, 0)
    left_basis = lax.dot_general(
        power_row, mine, (((1,), (1,)), ((), ())), precision=HI, preferred_element_type=jnp.float32
    )
    return (left_stat, right_stat, left_basis)


def solution(mesh):
    return jax.shard_map(
        on_device,
        mesh=mesh,
        in_specs=(P("shard", "role"), P("shard", "role"), P("shard", "role"), P("shard", "role")),
        out_specs=(P("shard", "role"), P("shard", "role"), P("shard", "role")),
        check_vma=False,
    )
```

```python
import functools

import jax
import jax.numpy as jnp
from jax import lax
from jax.experimental import pallas as pl
from jax.experimental.pallas import tpu as pltpu
from jax.sharding import PartitionSpec as P

smoothing = 0.95
clip_ratio = 4.0
epsilon_value = 1e-06
HI = lax.Precision.HIGHEST
BLOCK, PANEL = 128, 8


def factor_block(t_ref):
    w = PANEL
    sub = lax.broadcasted_iota(jnp.int32, (w, 128), 0)
    full = lambda v: jnp.broadcast_to(v, (w, 128))
    for p in range(BLOCK // w):
        c0 = p * w
        left, right = t_ref[c0:c0 + w, 0:128], t_ref[c0:c0 + w, 128:256]
        cols = [full(left[:, c0 + k:c0 + k + 1]) for k in range(w)]
        e = {(i, k): full(cols[k][i:i + 1, :]) for i in range(w) for k in range(i + 1)}
        l, inv, rs = {}, [], []
        for j in range(w):
            r = 1.0 / e[j, j]
            inv.append(r); rs.append(lax.rsqrt(e[j, j]))
            for i in range(j + 1, w):
                l[i, j] = e[i, j] * r
            for i in range(j + 1, w):
                for k in range(j + 1, i + 1):
                    e[i, k] = e[i, k] - l[i, j] * e[k, j]
        li = {}
        for k in range(w):
            for i in range(k + 1, w):
                acc = l[i, k]
                for m in range(k + 1, i):
                    acc = acc + l[i, m] * li[m, k]
                li[i, k] = -acc

        def pick(vals):
            out = jnp.zeros((w, 128), jnp.float32)
            for i, v in vals.items():
                out = jnp.where(sub == i, v, out)
            return out

        zl, zr = left, right
        for k in range(w - 1):
            coef = pick({i: li[i, k] for i in range(k + 1, w)})
            zl = zl + coef * full(left[k:k + 1, :])
            zr = zr + coef * full(right[k:k + 1, :])
        dinv = pick(dict(enumerate(inv)))
        ul, ur = dinv * zl, dinv * zr
        vl, vr = ul, ur
        for k in range(1, w):
            coef = pick({i: li[k, i] for i in range(k)})
            vl = vl + coef * full(ul[k:k + 1, :])
            vr = vr + coef * full(ur[k:k + 1, :])
        vlb = [full(vl[k:k + 1, :]) for k in range(w)]
        vrb = [full(vr[k:k + 1, :]) for k in range(w)]
        for q in range(p + 1, BLOCK // w):
            rows = slice(q * w, q * w + w)
            al, ar = t_ref[rows, 0:128], t_ref[rows, 128:256]
            nl, nr = al, ar
            for k in range(w):
                a = full(al[:, c0 + k:c0 + k + 1])
                nl = nl - a * vlb[k]
                nr = nr - a * vrb[k]
            t_ref[rows, 0:128] = nl
            t_ref[rows, 128:256] = nr
        scale = pick(dict(enumerate(rs)))
        t_ref[c0:c0 + w, 0:128] = scale * zl
        t_ref[c0:c0 + w, 128:256] = scale * zr


def strip_of(order, roles, role, which):
    height = order // (2 * roles)
    strip = role if which == 0 else 2 * roles - 1 - role
    return strip * height, height, strip * height // BLOCK * BLOCK


def packed_width(order, roles):
    return max(
        sum(order - strip_of(order, roles, role, which)[2] for which in (0, 1)) for role in range(roles)
    )


def gram_kernel(roles, power_ref, out_ref):
    order = power_ref.shape[1]
    here = lax.axis_index("role")
    for role in range(roles):

        @pl.when(here == role)
        def _():
            at = 0
            for which in (0, 1):
                row, height, first = strip_of(order, roles, role, which)
                out_ref[:, at : at + order - first] = lax.dot_general(
                    power_ref[:, row : row + height],
                    power_ref[:, first:],
                    (((0,), (0,)), ((), ())),
                    precision=HI,
                    preferred_element_type=jnp.float32,
                )
                at += order - first
            if at < out_ref.shape[1]:
                out_ref[:, at:] = jnp.zeros((out_ref.shape[0], out_ref.shape[1] - at), jnp.float32)


def basis_kernel(roles, packed_ref, power_ref, out_ref, m_ref, t_ref):
    n = power_ref.shape[1]
    nb = n // BLOCK
    for role in range(roles):
        at = 0
        for which in (0, 1):
            row, height, first = strip_of(n, roles, role, which)
            m_ref[row : row + height, first:n] = packed_ref[role, :, at : at + n - first]
            at += n - first
    m_ref[:, n:] = (
        lax.broadcasted_iota(jnp.int32, (n, n), 0) == lax.broadcasted_iota(jnp.int32, (n, n), 1)
    ).astype(jnp.float32)

    @pl.loop(0, nb)
    def _(b):
        start = pl.multiple_of(b * BLOCK, BLOCK)
        t_ref[:, :BLOCK] = m_ref[pl.ds(start, BLOCK), pl.ds(start, BLOCK)]
        t_ref[:, BLOCK:] = (
            lax.broadcasted_iota(jnp.int32, (BLOCK, BLOCK), 0)
            == lax.broadcasted_iota(jnp.int32, (BLOCK, BLOCK), 1)
        ).astype(jnp.float32)
        factor_block(t_ref)
        for c in range(nb):

            @pl.when(b == c)
            def _():
                lo, hi = c * BLOCK, n + (c + 1) * BLOCK
                rows = jnp.dot(
                    t_ref[:, BLOCK:],
                    m_ref[lo : lo + BLOCK, lo:hi],
                    precision=HI,
                    preferred_element_type=jnp.float32,
                )
                m_ref[lo : lo + BLOCK, lo:hi] = rows
                if c + 1 < nb:
                    m_ref[lo + BLOCK :, lo + BLOCK : hi] -= lax.dot_general(
                        rows[:, BLOCK : n - lo],
                        rows[:, BLOCK:],
                        (((0,), (0,)), ((), ())),
                        precision=HI,
                        preferred_element_type=jnp.float32,
                    )

    width = out_ref.shape[1]
    mine = pl.multiple_of(lax.axis_index("role") * width, BLOCK)
    out_ref[...] = lax.dot_general(
        power_ref[...],
        m_ref[pl.ds(mine, width), n:],
        (((1,), (1,)), ((), ())),
        precision=HI,
        preferred_element_type=jnp.float32,
    )


def split_three(value):
    high = lax.reduce_precision(value, 8, 7)
    rest = value - high
    middle = lax.reduce_precision(rest, 8, 7)
    return [v.astype(jnp.bfloat16) for v in (high, middle, rest - middle)]


def step(gradient, left_old, right_old, basis_old):
    rows, cols = gradient.shape
    vec = basis_old.shape[1]
    shards, roles = lax.axis_size("shard"), lax.axis_size("role")
    shard_at, role_at = lax.axis_index("shard"), lax.axis_index("role")
    order_size, order = rows * shards, vec * roles
    line = shards // 2
    line_at, side_at = shard_at // 2, shard_at % 2
    core_at = role_at % 2
    half_at = role_at // 2

    def other_side(value, first=0, last=line - 1):
        pairs = [(2 * z + x, 2 * z + 1 - x) for z in range(first, last + 1) for x in (0, 1)]
        return lax.ppermute(value, "shard", pairs)

    def along(value, first, last, by):
        pairs = [(2 * z + x, 2 * (z + by) + x) for z in range(first, last + 1) for x in (0, 1)]
        return lax.ppermute(value, "shard", pairs)

    def around(value, by):
        pairs = [(2 * z + x, 2 * ((z + by) % line) + x) for z in range(line) for x in (0, 1)]
        return lax.ppermute(value, "shard", pairs)

    def flip(value, axis, size, bit):
        return lax.ppermute(value, axis, [(i, i ^ bit) for i in range(size)])

    other_core = lambda value: flip(value, "role", roles, 1)
    other_half = lambda value: flip(value, "role", roles, 2)

    wide = gradient.astype(jnp.float32)
    parts = split_three(jnp.sum(wide * wide))
    tail = jnp.concatenate(
        [jnp.broadcast_to(v, (1, vec)) for v in parts] + [jnp.zeros((16 - len(parts), vec), jnp.bfloat16)]
    )
    message = jnp.concatenate([basis_old, tail])
    height = message.shape[0]
    beside = other_side(message)
    pair = jnp.where(side_at == 0, jnp.stack([message, beside]), jnp.stack([beside, message]))
    mine = lax.dynamic_update_slice(
        jnp.zeros((line, 2, height, vec), jnp.bfloat16), pair[None], (line_at, 0, 0, 0)
    )
    for by in range(1, line):
        got = around(pair, by)
        mine = lax.dynamic_update_slice(mine, got[None], ((line_at - by) % line, 0, 0, 0))
    yours = other_half(mine)
    two = jnp.where(
        half_at == 0, jnp.stack([mine, yours], axis=3), jnp.stack([yours, mine], axis=3)
    )
    their = other_core(two)
    four = jnp.where(
        core_at == 0, jnp.stack([two, their], axis=4), jnp.stack([their, two], axis=4)
    ).reshape(shards, height, order)
    sums = four[:, rows : rows + len(parts)].reshape(shards, len(parts), roles, vec)[..., 0]
    squares = jnp.sum(jnp.sum(sums.astype(jnp.float32), axis=1))
    factor = jnp.minimum(
        1.0, clip_ratio * jnp.sqrt(jnp.float32(order_size)) / jnp.sqrt(squares + epsilon_value)
    )
    weight = (1.0 - smoothing) * (factor * factor)
    basis = four[:, :rows]

    gathered = jnp.zeros((shards + 1, rows, cols), jnp.bfloat16)

    def put(gathered, value, z, x, valid):
        place = jnp.where(valid, 2 * z + x, shards)
        return lax.dynamic_update_slice(gathered, value[None], (place, 0, 0))

    gathered = put(gathered, gradient, line_at, side_at, True)
    low = high = gradient
    gathered = put(gathered, other_side(gradient), line_at, 1 - side_at, True)
    for by in range(1, line):
        low = along(low, by - 1, line - 2, 1)
        high = along(high, 1, line - by, -1)
        low_side = other_side(low, by, line - 1)
        high_side = other_side(high, 0, line - 1 - by)
        for value, z, x, valid in (
            (low, line_at - by, side_at, line_at >= by),
            (high, line_at + by, side_at, line_at + by < line),
            (low_side, line_at - by, 1 - side_at, line_at >= by),
            (high_side, line_at + by, 1 - side_at, line_at + by < line),
        ):
            gathered = put(gathered, value, z, x, valid)
    columns = gathered[:shards].reshape(order_size, cols)

    turned = lax.dot_general(
        columns,
        basis.reshape(order_size, order),
        (((0,), (0,)), ((), ())),
        preferred_element_type=jnp.float32,
    )
    per_role = cols // rows
    old_part = jnp.dot(
        left_old,
        lax.dynamic_slice_in_dim(basis, role_at * per_role, per_role, 0)
        .reshape(cols, order)
        .astype(jnp.float32),
        precision=HI,
    )
    new_part = sum(
        jnp.dot(gradient, part, preferred_element_type=jnp.float32) for part in split_three(turned)
    )
    part = smoothing * old_part + weight * new_part
    half_rows = rows // 2
    keep = lax.dynamic_slice_in_dim(part, core_at * half_rows, half_rows, 0)
    send = lax.dynamic_slice_in_dim(part, (1 - core_at) * half_rows, half_rows, 0)
    keep = keep + other_core(send)
    keep = keep + other_half(keep)
    across = other_core(keep)
    power = jnp.where(
        core_at == 0, jnp.concatenate([keep, across]), jnp.concatenate([across, keep])
    )

    strip_height = order // (2 * roles)
    packed = pl.pallas_call(
        functools.partial(gram_kernel, roles),
        out_shape=jax.ShapeDtypeStruct((strip_height, packed_width(order, roles)), jnp.float32),
    )(power)
    bit = 1
    while bit < shards:
        packed = packed + flip(packed, "shard", shards, bit)
        bit *= 2
    yours = other_half(packed)
    two = jnp.where(half_at == 0, jnp.stack([packed, yours]), jnp.stack([yours, packed]))
    their = other_core(two)
    strips = jnp.where(
        core_at == 0, jnp.stack([two, their], axis=1), jnp.stack([their, two], axis=1)
    ).reshape(roles, *packed.shape)
    left_basis = pl.pallas_call(
        functools.partial(basis_kernel, roles),
        out_shape=jax.ShapeDtypeStruct((rows, vec), jnp.float32),
        scratch_shapes=[
            pltpu.VMEM((order, 2 * order), jnp.float32),
            pltpu.VMEM((BLOCK, 2 * BLOCK), jnp.float32),
        ],
    )(strips, power)

    def left_for(half, core):
        at = (2 * half + core) * per_role
        block = lax.dynamic_slice_in_dim(gathered, at, per_role, 0).reshape(cols, cols)
        return lax.dot_general(
            gradient, block, (((1,), (1,)), ((), ())), preferred_element_type=jnp.float32
        )

    away = left_for(1 - half_at, core_at) + other_core(left_for(1 - half_at, 1 - core_at))
    here = left_for(half_at, core_at) + other_core(left_for(half_at, 1 - core_at))
    left_stat = smoothing * left_old + weight * (here + other_half(away))

    owner_of = lambda shard: shard * rows // cols
    owner = owner_of(shard_at)
    slab = lax.dynamic_slice_in_dim(columns, shard_at * rows - owner * cols, rows, 1)
    flat = lambda role, shard: role * shards + shard
    crossed = lax.ppermute(
        slab, ("role", "shard"),
        [(flat(owner_of(s), s), flat(owner_of(s) ^ 2, s)) for s in range(shards)],
    )
    slab = jnp.where(role_at == owner, slab, crossed)
    beside = lax.ppermute(
        slab, ("role", "shard"),
        [(flat(owner_of(s) ^ k, s), flat(owner_of(s) ^ k ^ 1, s)) for s in range(shards) for k in (0, 2)],
    )
    slab = jnp.where((role_at ^ owner) & 1 == 0, slab, beside)
    right_gram = lax.dot_general(
        slab, columns, (((0,), (0,)), ((), ())), preferred_element_type=jnp.float32
    )
    right_stat = smoothing * right_old + weight * right_gram
    return (left_stat, right_stat, left_basis)


def solution(mesh):
    return jax.shard_map(
        step,
        mesh=mesh,
        in_specs=(P("shard", "role"), P("shard", "role"), P("shard", "role"), P("shard", "role")),
        out_specs=(P("shard", "role"), P("shard", "role"), P("shard", "role")),
        check_vma=False,
    )
```

```python
import functools

import jax
import jax.numpy as jnp
from jax import lax
from jax.experimental import pallas as pl
from jax.experimental.pallas import tpu as pltpu
from jax.sharding import PartitionSpec as P

smoothing = 0.95
clip_ratio = 4.0
epsilon_value = 1e-06
HI = lax.Precision.HIGHEST
BLOCK, PANEL = 128, 8


def factor_block(t_ref):
    w = PANEL
    sub = lax.broadcasted_iota(jnp.int32, (w, 128), 0)
    full = lambda v: jnp.broadcast_to(v, (w, 128))
    for p in range(BLOCK // w):
        c0 = p * w
        left, right = t_ref[c0:c0 + w, 0:128], t_ref[c0:c0 + w, 128:256]
        cols = [full(left[:, c0 + k:c0 + k + 1]) for k in range(w)]
        e = {(i, k): full(cols[k][i:i + 1, :]) for i in range(w) for k in range(i + 1)}
        l, inv, rs = {}, [], []
        for j in range(w):
            r = 1.0 / e[j, j]
            inv.append(r); rs.append(lax.rsqrt(e[j, j]))
            for i in range(j + 1, w):
                l[i, j] = e[i, j] * r
            for i in range(j + 1, w):
                for k in range(j + 1, i + 1):
                    e[i, k] = e[i, k] - l[i, j] * e[k, j]
        li = {}
        for k in range(w):
            for i in range(k + 1, w):
                acc = l[i, k]
                for m in range(k + 1, i):
                    acc = acc + l[i, m] * li[m, k]
                li[i, k] = -acc

        def pick(vals):
            out = jnp.zeros((w, 128), jnp.float32)
            for i, v in vals.items():
                out = jnp.where(sub == i, v, out)
            return out

        zl, zr = left, right
        for k in range(w - 1):
            coef = pick({i: li[i, k] for i in range(k + 1, w)})
            zl = zl + coef * full(left[k:k + 1, :])
            zr = zr + coef * full(right[k:k + 1, :])
        dinv = pick(dict(enumerate(inv)))
        ul, ur = dinv * zl, dinv * zr
        vl, vr = ul, ur
        for k in range(1, w):
            coef = pick({i: li[k, i] for i in range(k)})
            vl = vl + coef * full(ul[k:k + 1, :])
            vr = vr + coef * full(ur[k:k + 1, :])
        vlb = [full(vl[k:k + 1, :]) for k in range(w)]
        vrb = [full(vr[k:k + 1, :]) for k in range(w)]
        for q in range(p + 1, BLOCK // w):
            rows = slice(q * w, q * w + w)
            al, ar = t_ref[rows, 0:128], t_ref[rows, 128:256]
            nl, nr = al, ar
            for k in range(w):
                a = full(al[:, c0 + k:c0 + k + 1])
                nl = nl - a * vlb[k]
                nr = nr - a * vrb[k]
            t_ref[rows, 0:128] = nl
            t_ref[rows, 128:256] = nr
        scale = pick(dict(enumerate(rs)))
        t_ref[c0:c0 + w, 0:128] = scale * zl
        t_ref[c0:c0 + w, 128:256] = scale * zr


GRANT = {"message": 8, "parts": 20, "power": 24, "gram": 12, "basis": 16, "sides": 24, "right": 20}


def strip_of(order, roles, role, which):
    height = order // (2 * roles)
    strip = role if which == 0 else 2 * roles - 1 - role
    return strip * height, height, strip * height // BLOCK * BLOCK


def packed_width(order, roles):
    return max(
        sum(order - strip_of(order, roles, role, which)[2] for which in (0, 1)) for role in range(roles)
    )


def product(a, b, contract, precision=None):
    return lax.dot_general(
        a, b, ((contract[:1], contract[1:]), ((), ())), precision=precision, preferred_element_type=jnp.float32
    )


def eye(n):
    return (
        lax.broadcasted_iota(jnp.int32, (n, n), 0) == lax.broadcasted_iota(jnp.int32, (n, n), 1)
    ).astype(jnp.float32)


def rounded_parts(value):
    high = value.astype(jnp.bfloat16)
    rest = value - high.astype(jnp.float32)
    middle = rest.astype(jnp.bfloat16)
    return high, middle, (rest - middle.astype(jnp.float32)).astype(jnp.bfloat16)


def fetch(pieces, held, sems):
    line = held.shape[0]
    line_at = lax.axis_index("shard") // 2
    start = lambda ref, dz, dx: pltpu.make_async_copy(ref, held.at[dz, dx], sems.at[dz, dx]).start()
    start(pieces[0], 0, 0)
    start(pieces[1], 0, 1)
    for by in range(1, line):
        low, high, low_side, high_side = pieces[4 * by - 1 : 4 * by + 3]
        skip = 1 if by == 1 else 0

        @pl.when(line_at >= by)
        def _():
            start(low, by, 0)

        @pl.when(line_at >= by + skip)
        def _():
            start(low_side, by, 1)

        @pl.when(line_at + by < line)
        def _():
            start(high, line - by, 0)

        @pl.when(line_at + by + skip < line)
        def _():
            start(high_side, line - by, 1)

    @pl.when(line_at == 1)
    def _():
        start(pieces[2], 1, 1)

    @pl.when(line_at == line - 2)
    def _():
        start(pieces[2], line - 1, 1)

    def wait(dz):
        for dx in (0, 1):
            pltpu.make_async_copy(pieces[0], held.at[dz, dx], sems.at[dz, dx]).wait()

    return wait


def message_kernel(gradient_ref, basis_ref, out_ref):
    rows, vec = basis_ref.shape
    wide = gradient_ref[...].astype(jnp.float32)
    squares = jnp.broadcast_to(jnp.sum(jnp.sum(wide * wide, axis=0, keepdims=True), axis=1, keepdims=True), (16, vec))
    out_ref[:rows, :] = basis_ref[...]
    at = lax.broadcasted_iota(jnp.int32, (16, vec), 0)
    tail = jnp.zeros((16, vec), jnp.float32)
    for i, part in enumerate(rounded_parts(squares)):
        tail = jnp.where(at == i, part.astype(jnp.float32), tail)
    out_ref[rows:, :] = tail.astype(jnp.bfloat16)


def basis_parts_kernel(order_size, left_ref, *refs):
    given, (turned_ref, old_ref, weight_ref, rows_ref) = refs[:8], refs[8:]
    rows, cols = left_ref.shape
    line, _, vec = given[0].shape
    per_role = cols // rows
    shard_at, role_at = lax.axis_index("shard"), lax.axis_index("role")
    line_at, side_at = shard_at // 2, shard_at % 2
    total = jnp.zeros((1, vec), jnp.float32)
    for bits, refs in zip((0, 2, 1, 3), (given[0:2], given[2:4], given[4:6], given[6:8])):
        at = pl.multiple_of((role_at ^ bits) * vec, BLOCK)
        whole = jnp.concatenate([refs[dx][dz, :rows, :] for dz in range(line) for dx in (0, 1)])
        turned_ref[pl.ds(at, vec), :] = whole.astype(jnp.float32).T.astype(jnp.bfloat16)
        for i in range(per_role):
            shard = role_at * per_role + i
            dz = lax.rem(line_at - shard // 2 + line, line)
            for dx in (0, 1):

                @pl.when((shard + side_at) % 2 == dx)
                def _():
                    rows_ref[i * rows : (i + 1) * rows, pl.ds(at, vec)] = refs[dx][dz, :rows, :]

        for ref in refs:
            for dz in range(line):
                total = total + jnp.sum(ref[dz, rows:, :].astype(jnp.float32), axis=0, keepdims=True)
    factor = jnp.minimum(
        1.0, clip_ratio * jnp.sqrt(jnp.float32(order_size)) / jnp.sqrt(total + epsilon_value)
    )
    weight_ref[...] = jnp.broadcast_to((1.0 - smoothing) * (factor * factor), weight_ref.shape)
    old = jnp.zeros(old_ref.shape, jnp.float32)
    for part in rounded_parts(left_ref[...]):
        old = old + product(part, rows_ref[...], (1, 0))
    old_ref[...] = smoothing * old


def power_kernel(count, *refs):
    pieces, (turned_ref, old_ref, weight_ref, keep_ref, send_ref, held, part_ref, sems) = refs[:count], refs[count:]
    line, _, rows, cols = held.shape
    order = turned_ref.shape[0]
    wait = fetch(pieces, held, sems)
    for dz in range(line):
        wait(dz)
    turned = product(turned_ref[...], held[...].reshape(2 * line * rows, cols), (1, 0))
    own = held[0, 0]
    new = jnp.zeros((rows, order), jnp.float32)
    for part in rounded_parts(turned):
        new = new + product(own, part, (1, 1))
    part_ref[...] = old_ref[...] + weight_ref[0:1, 0:1] * new
    half = rows // 2
    core_at = lax.axis_index("role") % 2
    for core in (0, 1):

        @pl.when(core_at == core)
        def _():
            keep_ref[...] = part_ref[core * half : (core + 1) * half, :]
            send_ref[...] = part_ref[(1 - core) * half : (2 - core) * half, :]


def gram_kernel(roles, keep_ref, across_ref, out_ref, power_ref):
    order = power_ref.shape[1]
    half = keep_ref.shape[0]
    here = lax.axis_index("role")
    for core in (0, 1):

        @pl.when(here % 2 == core)
        def _():
            power_ref[core * half : (core + 1) * half, :] = keep_ref[...]
            power_ref[(1 - core) * half : (2 - core) * half, :] = across_ref[...]

    for role in range(roles):

        @pl.when(here == role)
        def _():
            at = 0
            for which in (0, 1):
                row, height, first = strip_of(order, roles, role, which)
                out_ref[:, at : at + order - first] = product(
                    power_ref[:, row : row + height], power_ref[:, first:], (0, 0), HI
                )
                at += order - first
            if at < out_ref.shape[1]:
                out_ref[:, at:] = jnp.zeros((out_ref.shape[0], out_ref.shape[1] - at), jnp.float32)


def basis_kernel(roles, *refs):
    given, (power_ref, out_ref, m_ref, t_ref) = refs[:4], refs[4:]
    n = power_ref.shape[1]
    nb = n // BLOCK
    here = lax.axis_index("role")
    for bits, ref in zip((0, 2, 1, 3), given):
        for role in range(roles):

            @pl.when(here ^ bits == role)
            def _():
                at = 0
                for which in (0, 1):
                    row, height, first = strip_of(n, roles, role, which)
                    m_ref[row : row + height, first:n] = ref[:, at : at + n - first]
                    at += n - first

    m_ref[:, n:] = eye(n)

    @pl.loop(0, nb)
    def _(b):
        start = pl.multiple_of(b * BLOCK, BLOCK)
        t_ref[:, :BLOCK] = m_ref[pl.ds(start, BLOCK), pl.ds(start, BLOCK)]
        t_ref[:, BLOCK:] = eye(BLOCK)
        factor_block(t_ref)
        for c in range(nb):

            @pl.when(b == c)
            def _():
                lo, hi = c * BLOCK, n + (c + 1) * BLOCK
                rows = jnp.dot(
                    t_ref[:, BLOCK:],
                    m_ref[lo : lo + BLOCK, lo:hi],
                    precision=HI,
                    preferred_element_type=jnp.float32,
                )
                m_ref[lo : lo + BLOCK, lo:hi] = rows
                if c + 1 < nb:
                    m_ref[lo + BLOCK :, lo + BLOCK : hi] -= lax.dot_general(
                        rows[:, BLOCK : n - lo],
                        rows[:, BLOCK:],
                        (((0,), (0,)), ((), ())),
                        precision=HI,
                        preferred_element_type=jnp.float32,
                    )

    width = out_ref.shape[1]
    mine = pl.multiple_of(here * width, BLOCK)
    out_ref[...] = product(power_ref[...], m_ref[pl.ds(mine, width), n:], (1, 1), HI)


def sides_kernel(count, *refs):
    pieces, outs, (slab_ref, held, block_ref, sems) = refs[:count], refs[count:-4], refs[-4:]
    line, _, rows, cols = held.shape
    per_role = cols // rows
    shard_at, role_at = lax.axis_index("shard"), lax.axis_index("role")
    line_at, side_at = shard_at // 2, shard_at % 2
    wait = fetch(pieces, held, sems)
    for dz in range(line):
        wait(dz)
    own = held[0, 0]
    for bits, out in zip((3, 1, 2, 0), outs):
        for i in range(per_role):
            shard = (role_at ^ bits) * per_role + i
            dz = lax.rem(line_at - shard // 2 + line, line)
            block_ref[i * rows : (i + 1) * rows, :] = held[dz, (shard + side_at) % 2]
        out[...] = product(own, block_ref[...], (1, 1))
    for i in range(per_role):

        @pl.when(shard_at % per_role == i)
        def _():
            slab = held[:, :, :, i * rows : (i + 1) * rows].reshape(2 * line * rows, rows)
            slab_ref[...] = slab.astype(jnp.float32).T.astype(jnp.bfloat16)


def right_kernel(count, *refs):
    pieces, slabs = refs[:count], refs[count : count + 4]
    old_ref, weight_ref, out_ref, held, slab, sems, slab_sem = refs[count + 4 :]
    line, _, rows, cols = held.shape
    owner = lax.axis_index("shard") * rows // cols
    wait = fetch(pieces, held, sems)
    for bits, ref in enumerate(slabs):

        @pl.when(lax.axis_index("role") ^ owner == bits)
        def _():
            pltpu.make_async_copy(ref, slab, slab_sem).start()

    pltpu.make_async_copy(slabs[0], slab, slab_sem).wait()
    for dz in range(line):
        wait(dz)
    gram = product(slab[...], held[...].reshape(2 * line * rows, cols), (1, 0))
    out_ref[...] = smoothing * old_ref[...] + weight_ref[0:1, 0:1] * gram


def step(gradient, left_old, right_old, basis_old):
    rows, cols = gradient.shape
    vec = basis_old.shape[1]
    shards, roles = lax.axis_size("shard"), lax.axis_size("role")
    order_size, order = rows * shards, vec * roles
    line = shards // 2

    def other_side(value, first=0, last=line - 1):
        pairs = [(2 * z + x, 2 * z + 1 - x) for z in range(first, last + 1) for x in (0, 1)]
        return lax.ppermute(value, "shard", pairs)

    def along(value, first, last, by):
        pairs = [(2 * z + x, 2 * (z + by) + x) for z in range(first, last + 1) for x in (0, 1)]
        return lax.ppermute(value, "shard", pairs)

    def around(value, by):
        pairs = [(2 * z + x, 2 * ((z + by) % line) + x) for z in range(line) for x in (0, 1)]
        return lax.ppermute(value, "shard", pairs)

    def flip(value, axis, size, bit):
        return lax.ppermute(value, axis, [(i, i ^ bit) for i in range(size)])

    other_core = lambda value: flip(value, "role", roles, 1)
    other_half = lambda value: flip(value, "role", roles, 2)

    side = other_side(gradient)
    inward = [(2 * z + x, 2 * to + x) for z, to in ((0, 1), (line - 1, line - 2)) for x in (0, 1)]
    pieces = [gradient, side, lax.ppermute(side, "shard", inward)]
    low = high = gradient
    for by in range(1, line):
        low = along(low, by - 1, line - 2, 1)
        high = along(high, 1, line - by, -1)
        pieces += [low, high]
        skip = 1 if by == 1 else 0
        pieces.append(other_side(low, by + skip, line - 1))
        pieces.append(other_side(high, 0, line - 1 - by - skip))

    def call(name, kernel, out_shape, **options):
        return pl.pallas_call(
            kernel,
            out_shape=out_shape,
            compiler_params=pltpu.CompilerParams(vmem_limit_bytes=GRANT[name] << 20),
            **options,
        )

    anywhere = pl.BlockSpec(memory_space=pl.ANY)
    in_vmem = pl.BlockSpec(memory_space=pltpu.VMEM)
    count = len(pieces)
    held = pltpu.VMEM((line, 2, rows, cols), jnp.bfloat16)
    sems = pltpu.SemaphoreType.DMA((line, 2))
    shape = lambda *dims, dtype=jnp.float32: jax.ShapeDtypeStruct(dims, dtype)

    message = call("message", message_kernel, shape(rows + 16, vec, dtype=jnp.bfloat16))(gradient, basis_old)
    column = jnp.stack([message] + [around(message, by) for by in range(1, line)])
    across = other_side(column)
    mine = [column, across]
    yours = [other_half(column), other_half(across)]
    theirs = [other_core(value) for value in mine + yours]
    turned, old_part, weight = call(
        "parts",
        functools.partial(basis_parts_kernel, order_size),
        (shape(order, order_size, dtype=jnp.bfloat16), shape(rows, order), shape(8, BLOCK)),
        scratch_shapes=[pltpu.VMEM((cols, order), jnp.bfloat16)],
    )(left_old, *mine, *yours, *theirs)

    half_rows = rows // 2
    keep, send = call(
        "power",
        functools.partial(power_kernel, count),
        out_shape=(shape(half_rows, order), shape(half_rows, order)),
        in_specs=[anywhere] * count + [in_vmem] * 3,
        scratch_shapes=[held, pltpu.VMEM((rows, order), jnp.float32), sems],
    )(*pieces, turned, old_part, weight)
    keep = keep + other_core(send)
    keep = keep + other_half(keep)

    packed, power = call(
        "gram",
        functools.partial(gram_kernel, roles),
        out_shape=(shape(order // (2 * roles), packed_width(order, roles)), shape(rows, order)),
    )(keep, other_core(keep))
    bit = 1
    while bit < shards:
        packed = packed + flip(packed, "shard", shards, bit)
        bit *= 2
    yours = other_half(packed)
    left_basis = call(
        "basis",
        functools.partial(basis_kernel, roles),
        out_shape=shape(rows, vec),
        scratch_shapes=[
            pltpu.VMEM((order, 2 * order), jnp.float32),
            pltpu.VMEM((BLOCK, 2 * BLOCK), jnp.float32),
        ],
    )(packed, yours, other_core(packed), other_core(yours), power)

    *shares, slab = call(
        "sides",
        functools.partial(sides_kernel, count),
        out_shape=(shape(rows, cols),) * 4 + (shape(rows, order_size, dtype=jnp.bfloat16),),
        in_specs=[anywhere] * count,
        scratch_shapes=[held, pltpu.VMEM((cols, cols), jnp.bfloat16), sems],
    )(*pieces)
    away = shares[2] + other_core(shares[0])
    here = shares[3] + other_core(shares[1])
    left_stat = smoothing * left_old + weight[0, 0] * (here + other_half(away))

    owner_of = lambda shard: shard * rows // cols

    def from_owner(value, source, target):
        pairs = [
            tuple((owner_of(s) ^ bits) * shards + s for bits in (source, target)) for s in range(shards)
        ]
        return lax.ppermute(value, ("role", "shard"), pairs)

    crossed = from_owner(slab, 0, 2)
    right_stat = call(
        "right",
        functools.partial(right_kernel, count),
        out_shape=shape(rows, cols),
        in_specs=[anywhere] * (count + 4) + [in_vmem] * 2,
        scratch_shapes=[
            held,
            pltpu.VMEM((rows, order_size), jnp.bfloat16),
            sems,
            pltpu.SemaphoreType.DMA,
        ],
    )(*pieces, slab, from_owner(slab, 0, 1), crossed, from_owner(crossed, 2, 3), right_old, weight)
    return (left_stat, right_stat, left_basis)


def solution(mesh):
    return jax.shard_map(
        step,
        mesh=mesh,
        in_specs=(P("shard", "role"), P("shard", "role"), P("shard", "role"), P("shard", "role")),
        out_specs=(P("shard", "role"), P("shard", "role"), P("shard", "role")),
        check_vma=False,
    )
```

```python
import functools

import jax
import jax.numpy as jnp
from jax import lax
from jax.experimental import pallas as pl
from jax.experimental.pallas import tpu as pltpu
from jax.sharding import PartitionSpec as P

smoothing = 0.95
clip_ratio = 4.0
epsilon_value = 1e-06
HI = lax.Precision.HIGHEST
BLOCK, PANEL = 128, 8


def factor_block(sides, column_ref):
    w = PANEL
    sub = lax.broadcasted_iota(jnp.int32, (w, BLOCK), 0)
    full = lambda v: jnp.broadcast_to(v, (w, BLOCK))
    for p in range(BLOCK // w):
        c0 = p * w
        left = sides[0][c0 : c0 + w, :]
        cols = [full(left[:, c0 + k : c0 + k + 1]) for k in range(w)]
        for k in range(w):
            column_ref[k * w : k * w + w, :] = cols[k]
        e = {(i, k): column_ref[pl.ds(k * w + i, w, stride=0), :] for i in range(w) for k in range(i + 1)}
        rows = [[t[pl.ds(c0 + i, w, stride=0), :] for t in sides] for i in range(w)]
        l, inverse, root, done = {}, {}, [], [None] * w
        for j in range(0, w, 2):
            a, b, c = e[j, j], e[j + 1, j], e[j + 1, j + 1]
            r = 1.0 / (a * c - b * b)
            ar, br, cr = a * r, b * r, c * r
            inverse[j] = ar, br, cr
            slope = b / a
            root += [lax.rsqrt(a), lax.rsqrt(c - b * slope)]
            done[j] = rows[j]
            done[j + 1] = [y - slope * x for x, y in zip(rows[j], rows[j + 1])]
            for i in range(j + 2, w):
                x, y = e[i, j], e[i, j + 1]
                l[i, j], l[i, j + 1] = x * cr - y * br, y * ar - x * br
            for i in range(j + 2, w):
                for k in range(j + 2, i + 1):
                    e[i, k] = e[i, k] - (l[i, j] * e[k, j] + l[i, j + 1] * e[k, j + 1])
                rows[i] = [z - (l[i, j] * x + l[i, j + 1] * y) for x, y, z in zip(rows[j], rows[j + 1], rows[i])]
        for n, side in enumerate(sides):
            out = root[0] * done[0][n]
            for i in range(1, w):
                out = jnp.where(sub == i, root[i] * done[i][n], out)
            side[c0 : c0 + w, :] = out
        if c0 + w == BLOCK:
            break
        v = [None] * w
        for j in reversed(range(0, w, 2)):
            ar, br, cr = inverse[j]
            x, y = rows[j], rows[j + 1]
            v[j] = [cr * a - br * b for a, b in zip(x, y)]
            v[j + 1] = [ar * b - br * a for a, b in zip(x, y)]
            for k in (j, j + 1):
                for i in range(j + 2, w):
                    v[k] = [a - l[i, k] * b for a, b in zip(v[k], v[i])]
        for q in range(p + 1, BLOCK // w):
            at = slice(q * w, q * w + w)
            old = [t[at, :] for t in sides]
            c = [full(old[0][:, c0 + k : c0 + k + 1]) for k in range(w)]
            for n, side in enumerate(sides):
                terms = [c[k] * v[k][n] for k in range(w)]
                while len(terms) > 1:
                    terms = [a + b for a, b in zip(terms[::2], terms[1::2])]
                side[at, :] = old[n] - terms[0]


GRANT = {"message": 8, "parts": 20, "near": 24, "power": 24, "gram": 12, "basis": 16, "sides": 24, "right": 20, "left": 8, "last": 8}


def strip_of(order, roles, role, which):
    height = order // (2 * roles)
    strip = role if which == 0 else 2 * roles - 1 - role
    return strip * height, height, strip * height // BLOCK * BLOCK


def packed_width(order, roles):
    return max(
        sum(order - strip_of(order, roles, role, which)[2] for which in (0, 1)) for role in range(roles)
    )


def product(a, b, contract, precision=None):
    return lax.dot_general(
        a, b, ((contract[:1], contract[1:]), ((), ())), precision=precision, preferred_element_type=jnp.float32
    )


def eye(n):
    return (
        lax.broadcasted_iota(jnp.int32, (n, n), 0) == lax.broadcasted_iota(jnp.int32, (n, n), 1)
    ).astype(jnp.float32)


def rounded_parts(value):
    high = value.astype(jnp.bfloat16)
    rest = value - high.astype(jnp.float32)
    middle = rest.astype(jnp.bfloat16)
    return high, middle, (rest - middle.astype(jnp.float32)).astype(jnp.bfloat16)


def late_slots(line):
    line_at = lax.axis_index("shard") // 2
    return ((line_at >= line - 2, line - 2), (line_at < 2, 2))


def near_kernel(count, *refs):
    pieces, (turned_ref, held_ref, sum_ref, sems) = refs[:count], refs[count:]
    line, _, rows, cols = held_ref.shape
    line_at = lax.axis_index("shard") // 2
    side, inward, opposite, low_far, high_far = pieces[1:6]
    moves = [
        (pieces[0], 0, 0, line_at >= 0),
        (side, 0, 1, line_at >= 0),
        (inward, 1, 1, line_at == 1),
        (inward, line - 1, 1, line_at == line - 2),
        (opposite, 1, 1, line_at == 0),
        (opposite, line - 1, 1, line_at == line - 1),
        (high_far, 1, 0, line_at == 0),
        (low_far, line - 1, 0, line_at == line - 1),
    ]
    for by in range(1, line - 1):
        low, high, *sides = pieces[4 * by + 2 : 4 * by + 6]
        skip = 1 if by == 1 else 0
        moves += [(low, by, 0, line_at >= by), (high, line - by, 0, line_at + by < line)]
        if by < line - 2:
            moves += [
                (sides[0], by, 1, line_at >= by + skip),
                (sides[1], line - by, 1, line_at + by + skip < line),
            ]
    for start in (True, False):
        for n, (ref, dz, dx, when) in enumerate(moves):
            copy = pltpu.make_async_copy(ref, held_ref.at[dz, dx], sems.at[n])

            @pl.when(when)
            def _():
                copy.start() if start else copy.wait()

    sum_ref[...] = jnp.zeros_like(sum_ref)
    late = late_slots(line)
    for dz in range(line):
        missing = [when for when, slot in late if slot == dz]
        turned = lambda dx: turned_ref[:, (2 * dz + dx) * rows : (2 * dz + dx + 1) * rows]
        if not missing:
            sum_ref[...] += product(
                turned_ref[:, 2 * dz * rows : 2 * (dz + 1) * rows],
                held_ref[dz].reshape(2 * rows, cols),
                (1, 0),
            )
            continue
        sum_ref[...] += product(turned(0), held_ref[dz, 0], (1, 0))

        @pl.when(jnp.logical_not(functools.reduce(jnp.logical_or, missing)))
        def _():
            sum_ref[...] += product(turned(1), held_ref[dz, 1], (1, 0))


def message_kernel(gradient_ref, basis_ref, out_ref):
    rows, vec = basis_ref.shape
    wide = gradient_ref[...].astype(jnp.float32)
    squares = jnp.broadcast_to(jnp.sum(jnp.sum(wide * wide, axis=0, keepdims=True), axis=1, keepdims=True), (16, vec))
    out_ref[:rows, :] = basis_ref[...]
    at = lax.broadcasted_iota(jnp.int32, (16, vec), 0)
    tail = jnp.zeros((16, vec), jnp.float32)
    for i, part in enumerate(rounded_parts(squares)):
        tail = jnp.where(at == i, part.astype(jnp.float32), tail)
    out_ref[rows:, :] = tail.astype(jnp.bfloat16)


def basis_parts_kernel(order_size, left_ref, *refs):
    given, (turned_ref, old_ref, weight_ref, rows_ref) = refs[:8], refs[8:]
    rows, cols = left_ref.shape
    line, _, vec = given[0].shape
    per_role = cols // rows
    shard_at, role_at = lax.axis_index("shard"), lax.axis_index("role")
    line_at, side_at = shard_at // 2, shard_at % 2
    total = jnp.zeros((1, vec), jnp.float32)
    for bits, refs in zip((0, 2, 1, 3), (given[0:2], given[2:4], given[4:6], given[6:8])):
        at = pl.multiple_of((role_at ^ bits) * vec, BLOCK)
        whole = jnp.concatenate([refs[dx][dz, :rows, :] for dz in range(line) for dx in (0, 1)])
        turned_ref[pl.ds(at, vec), :] = whole.astype(jnp.float32).T.astype(jnp.bfloat16)
        for i in range(per_role):
            shard = role_at * per_role + i
            dz = lax.rem(line_at - shard // 2 + line, line)
            for dx in (0, 1):

                @pl.when((shard + side_at) % 2 == dx)
                def _():
                    rows_ref[i * rows : (i + 1) * rows, pl.ds(at, vec)] = refs[dx][dz, :rows, :]

        for ref in refs:
            for dz in range(line):
                total = total + jnp.sum(ref[dz, rows:, :].astype(jnp.float32), axis=0, keepdims=True)
    factor = jnp.minimum(
        1.0, clip_ratio * jnp.sqrt(jnp.float32(order_size)) / jnp.sqrt(total + epsilon_value)
    )
    weight_ref[...] = jnp.broadcast_to((1.0 - smoothing) * (factor * factor), weight_ref.shape)
    old = jnp.zeros(old_ref.shape, jnp.float32)
    for part in rounded_parts(left_ref[...]):
        old = old + product(part, rows_ref[...], (1, 0))
    old_ref[...] = smoothing * old


def power_kernel(low_ref, high_ref, held_in, sum_ref, turned_ref, old_ref, weight_ref, *refs):
    del held_in
    held_ref, keep_ref, send_ref, part_ref, total_ref, sem = refs
    line, _, rows, _ = held_ref.shape
    total_ref[...] = sum_ref[...]
    for (when, dz), ref in zip(late_slots(line), (low_ref, high_ref)):

        @pl.when(when)
        def _():
            copy = pltpu.make_async_copy(ref, held_ref.at[dz, 1], sem)
            copy.start()
            at = (2 * dz + 1) * rows
            total_ref[...] += product(turned_ref[:, at : at + rows], ref[...], (1, 0))
            copy.wait()

    own = held_ref[0, 0]
    new = jnp.zeros(part_ref.shape, jnp.float32)
    for part in rounded_parts(total_ref[...]):
        new = new + product(own, part, (1, 1))
    part_ref[...] = old_ref[...] + weight_ref[0:1, 0:1] * new
    half = rows // 2
    core_at = lax.axis_index("role") % 2
    for core in (0, 1):

        @pl.when(core_at == core)
        def _():
            keep_ref[...] = part_ref[core * half : (core + 1) * half, :]
            send_ref[...] = part_ref[(1 - core) * half : (2 - core) * half, :]


def gram_kernel(roles, keep_ref, across_ref, out_ref, power_ref):
    order = power_ref.shape[1]
    half = keep_ref.shape[0]
    here = lax.axis_index("role")
    for core in (0, 1):

        @pl.when(here % 2 == core)
        def _():
            power_ref[core * half : (core + 1) * half, :] = keep_ref[...]
            power_ref[(1 - core) * half : (2 - core) * half, :] = across_ref[...]

    for role in range(roles):

        @pl.when(here == role)
        def _():
            at = 0
            for which in (0, 1):
                row, height, first = strip_of(order, roles, role, which)
                out_ref[:, at : at + order - first] = product(
                    power_ref[:, row : row + height], power_ref[:, first:], (0, 0), HI
                )
                at += order - first
            if at < out_ref.shape[1]:
                out_ref[:, at:] = jnp.zeros((out_ref.shape[0], out_ref.shape[1] - at), jnp.float32)


def basis_kernel(roles, *refs):
    given, (power_ref, out_ref, m_ref, left_ref, right_ref, column_ref) = refs[:4], refs[4:]
    n = power_ref.shape[1]
    nb = n // BLOCK
    here = lax.axis_index("role")
    for bits, ref in zip((0, 2, 1, 3), given):
        for role in range(roles):

            @pl.when(here ^ bits == role)
            def _():
                at = 0
                for which in (0, 1):
                    row, height, first = strip_of(n, roles, role, which)
                    m_ref[row : row + height, first:n] = ref[:, at : at + n - first]
                    at += n - first

    m_ref[:, n:] = eye(n)

    down, along = [], []
    for c in range(nb):
        at = slice(c * BLOCK, (c + 1) * BLOCK)
        diagonal = jnp.where(eye(BLOCK) > 0, m_ref[at, at], 0.0)
        down.append(lax.rsqrt(jnp.sum(diagonal, axis=1, keepdims=True)))
        along.append(lax.rsqrt(jnp.sum(diagonal, axis=0, keepdims=True)))
    along = jnp.concatenate(along, axis=1)
    for c in range(nb):
        at = slice(c * BLOCK, (c + 1) * BLOCK)
        m_ref[at, c * BLOCK : n] = m_ref[at, c * BLOCK : n] * down[c] * along[:, c * BLOCK :]

    @pl.loop(0, nb)
    def _(b):
        start = pl.multiple_of(b * BLOCK, BLOCK)
        left_ref[...] = m_ref[pl.ds(start, BLOCK), pl.ds(start, BLOCK)]
        right_ref[...] = eye(BLOCK)
        factor_block((left_ref, right_ref), column_ref)
        for c in range(nb):

            @pl.when(b == c)
            def _():
                lo, hi = c * BLOCK, n + (c + 1) * BLOCK
                rows = right_ref[...]
                if nb > 1:
                    others = product(rows, m_ref[lo : lo + BLOCK, lo + BLOCK : hi - BLOCK], (1, 0), HI)
                    rows = jnp.concatenate([others, rows], axis=1)
                m_ref[lo : lo + BLOCK, lo + BLOCK : hi] = rows
                for d in range(c + 1, nb):
                    at = d * BLOCK
                    shift = (d - c - 1) * BLOCK
                    m_ref[at : at + BLOCK, at:hi] -= product(
                        rows[:, shift : shift + BLOCK], rows[:, shift:], (0, 0), HI
                    )

    width = out_ref.shape[1]
    mine = pl.multiple_of(here * width, BLOCK)
    out_ref[...] = product(power_ref[...], m_ref[pl.ds(mine, width), n:] * along, (1, 1), HI)


def sides_kernel(held_ref, *refs):
    *outs, slab_ref, block_ref = refs
    line, _, rows, cols = held_ref.shape
    per_role = cols // rows
    shard_at, role_at = lax.axis_index("shard"), lax.axis_index("role")
    line_at, side_at = shard_at // 2, shard_at % 2
    own = held_ref[0, 0]
    for bits, out in zip((3, 1, 2, 0), outs):
        for i in range(per_role):
            shard = (role_at ^ bits) * per_role + i
            dz = lax.rem(line_at - shard // 2 + line, line)
            block_ref[i * rows : (i + 1) * rows, :] = held_ref[dz, (shard + side_at) % 2]
        out[...] = product(own, block_ref[...], (1, 1))
    for i in range(per_role):

        @pl.when(shard_at % per_role == i)
        def _():
            slab = held_ref[:, :, :, i * rows : (i + 1) * rows].reshape(2 * line * rows, rows)
            slab_ref[...] = slab.astype(jnp.float32).T.astype(jnp.bfloat16)


def left_kernel(old_ref, own_ref, core_ref, weight_ref, out_ref):
    out_ref[...] = smoothing * old_ref[...] + weight_ref[0:1, 0:1] * (own_ref[...] + core_ref[...])


def last_kernel(sum_ref, half_ref, weight_ref, out_ref):
    out_ref[...] = sum_ref[...] + weight_ref[0:1, 0:1] * half_ref[...]


def right_kernel(held_ref, *refs):
    slabs, (old_ref, weight_ref, out_ref) = refs[:4], refs[4:]
    line, _, rows, cols = held_ref.shape
    owner = lax.axis_index("shard") * rows // cols
    for bits, ref in enumerate(slabs):

        @pl.when(lax.axis_index("role") ^ owner == bits)
        def _():
            gram = product(ref[...], held_ref[...].reshape(2 * line * rows, cols), (1, 0))
            out_ref[...] = smoothing * old_ref[...] + weight_ref[0:1, 0:1] * gram


def step(gradient, left_old, right_old, basis_old):
    rows, cols = gradient.shape
    vec = basis_old.shape[1]
    shards, roles = lax.axis_size("shard"), lax.axis_size("role")
    order_size, order = rows * shards, vec * roles
    line = shards // 2

    def other_side(value, first=0, last=line - 1):
        pairs = [(2 * z + x, 2 * z + 1 - x) for z in range(first, last + 1) for x in (0, 1)]
        return lax.ppermute(value, "shard", pairs)

    def along(value, first, last, by):
        pairs = [(2 * z + x, 2 * (z + by) + x) for z in range(first, last + 1) for x in (0, 1)]
        return lax.ppermute(value, "shard", pairs)

    def around(value, by):
        pairs = [(2 * z + x, 2 * ((z + by) % line) + x) for z in range(line) for x in (0, 1)]
        return lax.ppermute(value, "shard", pairs)

    def flip(value, axis, size, bit):
        return lax.ppermute(value, axis, [(i, i ^ bit) for i in range(size)])

    other_core = lambda value: flip(value, "role", roles, 1)
    other_half = lambda value: flip(value, "role", roles, 2)

    side = other_side(gradient)
    inward = [(2 * z + x, 2 * to + x) for z, to in ((0, 1), (line - 1, line - 2)) for x in (0, 1)]
    opposite = [(2 * z + x, 2 * (line - 1 - z) + x) for z in (0, line - 1) for x in (0, 1)]
    chain = []
    low = high = gradient
    for by in range(1, line):
        low = along(low, by - 1, line - 2, 1)
        high = along(high, 1, line - by, -1)
        chain += [low, high]
        if by < line - 1:
            skip = 1 if by == 1 else 0
            chain.append(other_side(low, by + skip, line - 1))
            chain.append(other_side(high, 0, line - 1 - by - skip))
    *chain, low_late, high_late, low_far, high_far = chain
    pieces = [
        gradient,
        side,
        lax.ppermute(side, "shard", inward),
        lax.ppermute(side, "shard", opposite),
        low_far,
        high_far,
        *chain,
    ]

    def call(name, kernel, out_shape, **options):
        return pl.pallas_call(
            kernel,
            out_shape=out_shape,
            compiler_params=pltpu.CompilerParams(vmem_limit_bytes=GRANT[name] << 20),
            **options,
        )

    anywhere = pl.BlockSpec(memory_space=pl.ANY)
    in_vmem = pl.BlockSpec(memory_space=pltpu.VMEM)
    shape = lambda *dims, dtype=jnp.float32: jax.ShapeDtypeStruct(dims, dtype)

    message = call("message", message_kernel, shape(rows + 16, vec, dtype=jnp.bfloat16))(gradient, basis_old)
    column = jnp.stack([message] + [around(message, by) for by in range(1, line)])
    across = other_side(column)
    mine = [column, across]
    yours = [other_half(column), other_half(across)]
    theirs = [other_core(value) for value in mine + yours]
    turned, old_part, weight = call(
        "parts",
        functools.partial(basis_parts_kernel, order_size),
        (shape(order, order_size, dtype=jnp.bfloat16), shape(rows, order), shape(8, BLOCK)),
        scratch_shapes=[pltpu.VMEM((cols, order), jnp.bfloat16)],
    )(left_old, *mine, *yours, *theirs)

    half_rows = rows // 2
    held, turned_sum = call(
        "near",
        functools.partial(near_kernel, len(pieces)),
        (shape(line, 2, rows, cols, dtype=jnp.bfloat16), shape(order, cols)),
        in_specs=[anywhere] * len(pieces) + [in_vmem],
        scratch_shapes=[pltpu.SemaphoreType.DMA((4 * line,))],
    )(*pieces, turned)
    held, keep, send = call(
        "power",
        power_kernel,
        (shape(line, 2, rows, cols, dtype=jnp.bfloat16), shape(half_rows, order), shape(half_rows, order)),
        in_specs=[in_vmem] * 7,
        input_output_aliases={2: 0},
        scratch_shapes=[
            pltpu.VMEM((rows, order), jnp.float32),
            pltpu.VMEM((order, cols), jnp.float32),
            pltpu.SemaphoreType.DMA,
        ],
    )(low_late, high_late, held, turned_sum, turned, old_part, weight)
    keep = keep + other_core(send)
    keep = keep + other_half(keep)

    packed, power = call(
        "gram",
        functools.partial(gram_kernel, roles),
        out_shape=(shape(order // (2 * roles), packed_width(order, roles)), shape(rows, order)),
    )(keep, other_core(keep))
    bit = 1
    while bit < shards:
        packed = packed + flip(packed, "shard", shards, bit)
        bit *= 2
    yours = other_half(packed)
    left_basis = call(
        "basis",
        functools.partial(basis_kernel, roles),
        out_shape=shape(rows, vec),
        scratch_shapes=[
            pltpu.VMEM((order, 2 * order), jnp.float32),
            pltpu.VMEM((BLOCK, BLOCK), jnp.float32),
            pltpu.VMEM((BLOCK, BLOCK), jnp.float32),
            pltpu.VMEM((PANEL * PANEL, BLOCK), jnp.float32),
        ],
    )(packed, yours, other_core(packed), other_core(yours), power)

    *shares, slab = call(
        "sides",
        sides_kernel,
        (shape(rows, cols),) * 4 + (shape(rows, order_size, dtype=jnp.bfloat16),),
        scratch_shapes=[pltpu.VMEM((cols, cols), jnp.bfloat16)],
    )(held)
    away = shares[2] + other_core(shares[0])
    left_sum = call("left", left_kernel, shape(rows, cols))(left_old, shares[3], other_core(shares[1]), weight)
    left_stat = call("last", last_kernel, shape(rows, cols))(left_sum, other_half(away), weight)
    owner_of = lambda shard: shard * rows // cols

    def from_owner(value, source, target):
        pairs = [
            tuple((owner_of(s) ^ bits) * shards + s for bits in (source, target)) for s in range(shards)
        ]
        return lax.ppermute(value, ("role", "shard"), pairs)

    crossed = from_owner(slab, 0, 2)
    right_stat = call("right", right_kernel, shape(rows, cols))(
        held, slab, from_owner(slab, 0, 1), crossed, from_owner(crossed, 2, 3), right_old, weight
    )
    return (left_stat, right_stat, left_basis)


def solution(mesh):
    return jax.shard_map(
        step,
        mesh=mesh,
        in_specs=(P("shard", "role"), P("shard", "role"), P("shard", "role"), P("shard", "role")),
        out_specs=(P("shard", "role"), P("shard", "role"), P("shard", "role")),
        check_vma=False,
    )
```

```python
import functools

import jax
import jax.numpy as jnp
from jax import lax
from jax.experimental import pallas as pl
from jax.experimental.pallas import tpu as pltpu
from jax.sharding import PartitionSpec as P

smoothing = 0.95
clip_ratio = 4.0
epsilon_value = 1e-06
HI = lax.Precision.HIGHEST
BLOCK, PANEL = 128, 8


def factor_block(sides, column_ref):
    w = PANEL
    sub = lax.broadcasted_iota(jnp.int32, (w, BLOCK), 0)
    full = lambda v: jnp.broadcast_to(v, (w, BLOCK))
    for p in range(BLOCK // w):
        c0 = p * w
        left = sides[0][c0 : c0 + w, :]
        cols = [full(left[:, c0 + k : c0 + k + 1]) for k in range(w)]
        for k in range(w):
            column_ref[k * w : k * w + w, :] = cols[k]
        e = {(i, k): column_ref[pl.ds(k * w + i, w, stride=0), :] for i in range(w) for k in range(i + 1)}
        rows = [[t[pl.ds(c0 + i, w, stride=0), :] for t in sides] for i in range(w)]
        l, inverse, root, done = {}, {}, [], [None] * w
        for j in range(0, w, 2):
            a, b, c = e[j, j], e[j + 1, j], e[j + 1, j + 1]
            r = 1.0 / (a * c - b * b)
            ar, br, cr = a * r, b * r, c * r
            inverse[j] = ar, br, cr
            slope = b / a
            root += [lax.rsqrt(a), lax.rsqrt(c - b * slope)]
            done[j] = rows[j]
            done[j + 1] = [y - slope * x for x, y in zip(rows[j], rows[j + 1])]
            for i in range(j + 2, w):
                x, y = e[i, j], e[i, j + 1]
                l[i, j], l[i, j + 1] = x * cr - y * br, y * ar - x * br
            for i in range(j + 2, w):
                for k in range(j + 2, i + 1):
                    e[i, k] = e[i, k] - (l[i, j] * e[k, j] + l[i, j + 1] * e[k, j + 1])
                rows[i] = [z - (l[i, j] * x + l[i, j + 1] * y) for x, y, z in zip(rows[j], rows[j + 1], rows[i])]
        for n, side in enumerate(sides):
            out = root[0] * done[0][n]
            for i in range(1, w):
                out = jnp.where(sub == i, root[i] * done[i][n], out)
            side[c0 : c0 + w, :] = out
        if c0 + w == BLOCK:
            break
        v = [None] * w
        for j in reversed(range(0, w, 2)):
            ar, br, cr = inverse[j]
            x, y = rows[j], rows[j + 1]
            v[j] = [cr * a - br * b for a, b in zip(x, y)]
            v[j + 1] = [ar * b - br * a for a, b in zip(x, y)]
            for k in (j, j + 1):
                for i in range(j + 2, w):
                    v[k] = [a - l[i, k] * b for a, b in zip(v[k], v[i])]
        for q in range(p + 1, BLOCK // w):
            at = slice(q * w, q * w + w)
            old = [t[at, :] for t in sides]
            c = [full(old[0][:, c0 + k : c0 + k + 1]) for k in range(w)]
            for n, side in enumerate(sides):
                terms = [c[k] * v[k][n] for k in range(w)]
                while len(terms) > 1:
                    terms = [a + b for a, b in zip(terms[::2], terms[1::2])]
                side[at, :] = old[n] - terms[0]


GRANT = {"message": 8, "parts": 20, "near": 24, "power": 24, "gram": 12, "basis": 16, "sides": 24, "right": 20, "left": 8, "last": 8}


def strip_of(order, roles, role, which):
    height = order // (2 * roles)
    strip = role if which == 0 else 2 * roles - 1 - role
    return strip * height, height, strip * height // BLOCK * BLOCK


def packed_width(order, roles):
    return max(
        sum(order - strip_of(order, roles, role, which)[2] for which in (0, 1)) for role in range(roles)
    )


def product(a, b, contract, precision=None):
    return lax.dot_general(
        a, b, ((contract[:1], contract[1:]), ((), ())), precision=precision, preferred_element_type=jnp.float32
    )


def eye(n):
    return (
        lax.broadcasted_iota(jnp.int32, (n, n), 0) == lax.broadcasted_iota(jnp.int32, (n, n), 1)
    ).astype(jnp.float32)


def rounded_parts(value):
    high = value.astype(jnp.bfloat16)
    rest = value - high.astype(jnp.float32)
    middle = rest.astype(jnp.bfloat16)
    return high, middle, (rest - middle.astype(jnp.float32)).astype(jnp.bfloat16)


def late_slots(line):
    line_at = lax.axis_index("shard") // 2
    return ((line_at >= line - 2, line - 2), (line_at < 2, 2))


def near_kernel(count, *refs):
    pieces, (turned_ref, held_ref, sum_ref, sems) = refs[:count], refs[count:]
    line, _, rows, cols = held_ref.shape
    line_at = lax.axis_index("shard") // 2
    side, inward, opposite, low_far, high_far = pieces[1:6]
    moves = [
        (pieces[0], 0, 0, line_at >= 0),
        (side, 0, 1, line_at >= 0),
        (inward, 1, 1, line_at == 1),
        (inward, line - 1, 1, line_at == line - 2),
        (opposite, 1, 1, line_at == 0),
        (opposite, line - 1, 1, line_at == line - 1),
        (high_far, 1, 0, line_at == 0),
        (low_far, line - 1, 0, line_at == line - 1),
    ]
    for by in range(1, line - 1):
        low, high, *sides = pieces[4 * by + 2 : 4 * by + 6]
        skip = 1 if by == 1 else 0
        moves += [(low, by, 0, line_at >= by), (high, line - by, 0, line_at + by < line)]
        if by < line - 2:
            moves += [
                (sides[0], by, 1, line_at >= by + skip),
                (sides[1], line - by, 1, line_at + by + skip < line),
            ]
    for start in (True, False):
        for n, (ref, dz, dx, when) in enumerate(moves):
            copy = pltpu.make_async_copy(ref, held_ref.at[dz, dx], sems.at[n])

            @pl.when(when)
            def _():
                copy.start() if start else copy.wait()

    sum_ref[...] = jnp.zeros_like(sum_ref)
    late = late_slots(line)
    for dz in range(line):
        missing = [when for when, slot in late if slot == dz]
        turned = lambda dx: turned_ref[:, (2 * dz + dx) * rows : (2 * dz + dx + 1) * rows]
        if not missing:
            sum_ref[...] += product(
                turned_ref[:, 2 * dz * rows : 2 * (dz + 1) * rows],
                held_ref[dz].reshape(2 * rows, cols),
                (1, 0),
            )
            continue
        sum_ref[...] += product(turned(0), held_ref[dz, 0], (1, 0))

        @pl.when(jnp.logical_not(functools.reduce(jnp.logical_or, missing)))
        def _():
            sum_ref[...] += product(turned(1), held_ref[dz, 1], (1, 0))


def message_kernel(gradient_ref, basis_ref, out_ref):
    rows, vec = basis_ref.shape
    wide = gradient_ref[...].astype(jnp.float32)
    squares = jnp.broadcast_to(jnp.sum(jnp.sum(wide * wide, axis=0, keepdims=True), axis=1, keepdims=True), (16, vec))
    out_ref[:rows, :] = basis_ref[...]
    at = lax.broadcasted_iota(jnp.int32, (16, vec), 0)
    tail = jnp.zeros((16, vec), jnp.float32)
    for i, part in enumerate(rounded_parts(squares)):
        tail = jnp.where(at == i, part.astype(jnp.float32), tail)
    out_ref[rows:, :] = tail.astype(jnp.bfloat16)


def basis_parts_kernel(order_size, left_ref, *refs):
    given, (turned_ref, old_ref, weight_ref, rows_ref) = refs[:8], refs[8:]
    rows, cols = left_ref.shape
    line, _, vec = given[0].shape
    per_role = cols // rows
    shard_at, role_at = lax.axis_index("shard"), lax.axis_index("role")
    line_at, side_at = shard_at // 2, shard_at % 2
    total = jnp.zeros((1, vec), jnp.float32)
    for bits, refs in zip((0, 2, 1, 3), (given[0:2], given[2:4], given[4:6], given[6:8])):
        at = pl.multiple_of((role_at ^ bits) * vec, BLOCK)
        whole = jnp.concatenate([refs[dx][dz, :rows, :] for dz in range(line) for dx in (0, 1)])
        turned_ref[pl.ds(at, vec), :] = whole.astype(jnp.float32).T.astype(jnp.bfloat16)
        for i in range(per_role):
            shard = role_at * per_role + i
            dz = lax.rem(line_at - shard // 2 + line, line)
            for dx in (0, 1):

                @pl.when((shard + side_at) % 2 == dx)
                def _():
                    rows_ref[i * rows : (i + 1) * rows, pl.ds(at, vec)] = refs[dx][dz, :rows, :]

        for ref in refs:
            for dz in range(line):
                total = total + jnp.sum(ref[dz, rows:, :].astype(jnp.float32), axis=0, keepdims=True)
    factor = jnp.minimum(
        1.0, clip_ratio * jnp.sqrt(jnp.float32(order_size)) / jnp.sqrt(total + epsilon_value)
    )
    weight_ref[...] = jnp.broadcast_to((1.0 - smoothing) * (factor * factor), weight_ref.shape)
    old = jnp.zeros(old_ref.shape, jnp.float32)
    for part in rounded_parts(left_ref[...]):
        old = old + product(part, rows_ref[...], (1, 0))
    old_ref[...] = smoothing * old


def power_kernel(low_ref, high_ref, held_in, sum_ref, turned_ref, old_ref, weight_ref, *refs):
    del held_in
    held_ref, keep_ref, send_ref, part_ref, total_ref, sem = refs
    line, _, rows, _ = held_ref.shape
    total_ref[...] = sum_ref[...]
    for (when, dz), ref in zip(late_slots(line), (low_ref, high_ref)):

        @pl.when(when)
        def _():
            copy = pltpu.make_async_copy(ref, held_ref.at[dz, 1], sem)
            copy.start()
            at = (2 * dz + 1) * rows
            total_ref[...] += product(turned_ref[:, at : at + rows], ref[...], (1, 0))
            copy.wait()

    own = held_ref[0, 0]
    new = jnp.zeros(part_ref.shape, jnp.float32)
    for part in rounded_parts(total_ref[...]):
        new = new + product(own, part, (1, 1))
    part_ref[...] = old_ref[...] + weight_ref[0:1, 0:1] * new
    half = rows // 2
    core_at = lax.axis_index("role") % 2
    for core in (0, 1):

        @pl.when(core_at == core)
        def _():
            keep_ref[...] = part_ref[core * half : (core + 1) * half, :]
            send_ref[...] = part_ref[(1 - core) * half : (2 - core) * half, :]


def gram_kernel(roles, keep_ref, across_ref, mine_ref, send_ref, power_ref):
    order = power_ref.shape[1]
    half = keep_ref.shape[0]
    here, side_at = lax.axis_index("role"), lax.axis_index("shard") % 2
    for core in (0, 1):

        @pl.when(here % 2 == core)
        def _():
            power_ref[core * half : (core + 1) * half, :] = keep_ref[...]
            power_ref[(1 - core) * half : (2 - core) * half, :] = across_ref[...]

    for role in range(roles):

        @pl.when(here == role)
        def _():
            at = 0
            for which in (0, 1):
                row, height, first = strip_of(order, roles, role, which)
                strip = product(power_ref[:, row : row + height], power_ref[:, first:], (0, 0), HI)
                parts = strip[: height // 2], strip[height // 2 :]
                for side in (0, 1):

                    @pl.when(side_at == side)
                    def _():
                        mine_ref[:, at : at + order - first] = parts[side]
                        send_ref[:, at : at + order - first] = parts[1 - side]

                at += order - first
            for ref in (mine_ref, send_ref):
                if at < ref.shape[1]:
                    ref[:, at:] = jnp.zeros((ref.shape[0], ref.shape[1] - at), jnp.float32)


def basis_kernel(roles, *refs):
    given, (power_ref, out_ref, m_ref, left_ref, right_ref, column_ref) = refs[:8], refs[8:]
    n = power_ref.shape[1]
    nb = n // BLOCK
    here, side_at = lax.axis_index("role"), lax.axis_index("shard") % 2
    for number, ref in enumerate(given):
        bits, side = ((0, 2, 1, 3)[number // 2], (side_at + number) % 2)
        for role in range(roles):

            @pl.when(here ^ bits == role)
            def _():
                at = 0
                for which in (0, 1):
                    row, height, first = strip_of(n, roles, role, which)
                    rows = pl.ds(pl.multiple_of(row + side * (height // 2), height // 2), height // 2)
                    m_ref[rows, first:n] = ref[:, at : at + n - first]
                    at += n - first

    m_ref[:, n:] = eye(n)

    down, along = [], []
    for c in range(nb):
        at = slice(c * BLOCK, (c + 1) * BLOCK)
        diagonal = jnp.where(eye(BLOCK) > 0, m_ref[at, at], 0.0)
        down.append(lax.rsqrt(jnp.sum(diagonal, axis=1, keepdims=True)))
        along.append(lax.rsqrt(jnp.sum(diagonal, axis=0, keepdims=True)))
    along = jnp.concatenate(along, axis=1)
    for c in range(nb):
        at = slice(c * BLOCK, (c + 1) * BLOCK)
        m_ref[at, c * BLOCK : n] = m_ref[at, c * BLOCK : n] * down[c] * along[:, c * BLOCK :]

    @pl.loop(0, nb)
    def _(b):
        start = pl.multiple_of(b * BLOCK, BLOCK)
        left_ref[...] = m_ref[pl.ds(start, BLOCK), pl.ds(start, BLOCK)]
        right_ref[...] = eye(BLOCK)
        factor_block((left_ref, right_ref), column_ref)
        for c in range(nb):

            @pl.when(b == c)
            def _():
                lo, hi = c * BLOCK, n + (c + 1) * BLOCK
                rows = right_ref[...]
                if nb > 1:
                    others = product(rows, m_ref[lo : lo + BLOCK, lo + BLOCK : hi - BLOCK], (1, 0), HI)
                    rows = jnp.concatenate([others, rows], axis=1)
                m_ref[lo : lo + BLOCK, lo + BLOCK : hi] = rows
                for d in range(c + 1, nb):
                    at = d * BLOCK
                    shift = (d - c - 1) * BLOCK
                    m_ref[at : at + BLOCK, at:hi] -= product(
                        rows[:, shift : shift + BLOCK], rows[:, shift:], (0, 0), HI
                    )

    width = out_ref.shape[1]
    mine = pl.multiple_of(here * width, BLOCK)
    out_ref[...] = product(power_ref[...], m_ref[pl.ds(mine, width), n:] * along, (1, 1), HI)


def sides_kernel(held_ref, *refs):
    *outs, slab_ref, block_ref = refs
    line, _, rows, cols = held_ref.shape
    per_role = cols // rows
    shard_at, role_at = lax.axis_index("shard"), lax.axis_index("role")
    line_at, side_at = shard_at // 2, shard_at % 2
    own = held_ref[0, 0]
    for bits, out in zip((3, 1, 2, 0), outs):
        for i in range(per_role):
            shard = (role_at ^ bits) * per_role + i
            dz = lax.rem(line_at - shard // 2 + line, line)
            block_ref[i * rows : (i + 1) * rows, :] = held_ref[dz, (shard + side_at) % 2]
        out[...] = product(own, block_ref[...], (1, 1))
    for i in range(per_role):

        @pl.when(shard_at % per_role == i)
        def _():
            slab = held_ref[:, :, :, i * rows : (i + 1) * rows].reshape(2 * line * rows, rows)
            slab_ref[...] = slab.astype(jnp.float32).T.astype(jnp.bfloat16)


def left_kernel(old_ref, own_ref, core_ref, weight_ref, out_ref):
    out_ref[...] = smoothing * old_ref[...] + weight_ref[0:1, 0:1] * (own_ref[...] + core_ref[...])


def last_kernel(sum_ref, half_ref, weight_ref, out_ref):
    out_ref[...] = sum_ref[...] + weight_ref[0:1, 0:1] * half_ref[...]


def right_kernel(held_ref, *refs):
    slabs, (old_ref, weight_ref, out_ref) = refs[:4], refs[4:]
    line, _, rows, cols = held_ref.shape
    owner = lax.axis_index("shard") * rows // cols
    for bits, ref in enumerate(slabs):

        @pl.when(lax.axis_index("role") ^ owner == bits)
        def _():
            gram = product(ref[...], held_ref[...].reshape(2 * line * rows, cols), (1, 0))
            out_ref[...] = smoothing * old_ref[...] + weight_ref[0:1, 0:1] * gram


def step(gradient, left_old, right_old, basis_old):
    rows, cols = gradient.shape
    vec = basis_old.shape[1]
    shards, roles = lax.axis_size("shard"), lax.axis_size("role")
    order_size, order = rows * shards, vec * roles
    line = shards // 2

    def other_side(value, first=0, last=line - 1):
        pairs = [(2 * z + x, 2 * z + 1 - x) for z in range(first, last + 1) for x in (0, 1)]
        return lax.ppermute(value, "shard", pairs)

    def along(value, first, last, by):
        pairs = [(2 * z + x, 2 * (z + by) + x) for z in range(first, last + 1) for x in (0, 1)]
        return lax.ppermute(value, "shard", pairs)

    def around(value, by):
        pairs = [(2 * z + x, 2 * ((z + by) % line) + x) for z in range(line) for x in (0, 1)]
        return lax.ppermute(value, "shard", pairs)

    def flip(value, axis, size, bit):
        return lax.ppermute(value, axis, [(i, i ^ bit) for i in range(size)])

    other_core = lambda value: flip(value, "role", roles, 1)
    other_half = lambda value: flip(value, "role", roles, 2)

    side = other_side(gradient)
    inward = [(2 * z + x, 2 * to + x) for z, to in ((0, 1), (line - 1, line - 2)) for x in (0, 1)]
    opposite = [(2 * z + x, 2 * (line - 1 - z) + x) for z in (0, line - 1) for x in (0, 1)]
    chain = []
    low = high = gradient
    for by in range(1, line):
        low = along(low, by - 1, line - 2, 1)
        high = along(high, 1, line - by, -1)
        chain += [low, high]
        if by < line - 1:
            skip = 1 if by == 1 else 0
            chain.append(other_side(low, by + skip, line - 1))
            chain.append(other_side(high, 0, line - 1 - by - skip))
    *chain, low_late, high_late, low_far, high_far = chain
    pieces = [
        gradient,
        side,
        lax.ppermute(side, "shard", inward),
        lax.ppermute(side, "shard", opposite),
        low_far,
        high_far,
        *chain,
    ]

    def call(name, kernel, out_shape, **options):
        return pl.pallas_call(
            kernel,
            out_shape=out_shape,
            compiler_params=pltpu.CompilerParams(vmem_limit_bytes=GRANT[name] << 20),
            **options,
        )

    anywhere = pl.BlockSpec(memory_space=pl.ANY)
    in_vmem = pl.BlockSpec(memory_space=pltpu.VMEM)
    shape = lambda *dims, dtype=jnp.float32: jax.ShapeDtypeStruct(dims, dtype)

    message = call("message", message_kernel, shape(rows + 16, vec, dtype=jnp.bfloat16))(gradient, basis_old)
    column = jnp.stack([message] + [around(message, by) for by in range(1, line)])
    across = other_side(column)
    mine = [column, across]
    yours = [other_half(column), other_half(across)]
    theirs = [other_core(value) for value in mine + yours]
    turned, old_part, weight = call(
        "parts",
        functools.partial(basis_parts_kernel, order_size),
        (shape(order, order_size, dtype=jnp.bfloat16), shape(rows, order), shape(8, BLOCK)),
        scratch_shapes=[pltpu.VMEM((cols, order), jnp.bfloat16)],
    )(left_old, *mine, *yours, *theirs)

    half_rows = rows // 2
    held, turned_sum = call(
        "near",
        functools.partial(near_kernel, len(pieces)),
        (shape(line, 2, rows, cols, dtype=jnp.bfloat16), shape(order, cols)),
        in_specs=[anywhere] * len(pieces) + [in_vmem],
        scratch_shapes=[pltpu.SemaphoreType.DMA((4 * line,))],
    )(*pieces, turned)
    held, keep, send = call(
        "power",
        power_kernel,
        (shape(line, 2, rows, cols, dtype=jnp.bfloat16), shape(half_rows, order), shape(half_rows, order)),
        in_specs=[in_vmem] * 7,
        input_output_aliases={2: 0},
        scratch_shapes=[
            pltpu.VMEM((rows, order), jnp.float32),
            pltpu.VMEM((order, cols), jnp.float32),
            pltpu.SemaphoreType.DMA,
        ],
    )(low_late, high_late, held, turned_sum, turned, old_part, weight)
    keep = keep + other_core(send)
    keep = keep + other_half(keep)

    piece = shape(order // (4 * roles), packed_width(order, roles))
    packed, send, power = call("gram", functools.partial(gram_kernel, roles), (piece, piece, shape(rows, order)))(
        keep, other_core(keep)
    )
    packed = packed + other_side(send)
    bit = 2
    while bit < shards:
        packed = packed + flip(packed, "shard", shards, bit)
        bit *= 2
    slanted = [
        (role * shards + shard, (role ^ 2) * shards + (shard ^ 1))
        for role in range(roles)
        for shard in range(shards)
    ]
    mine = [packed, other_side(packed), other_half(packed), lax.ppermute(packed, ("role", "shard"), slanted)]
    theirs = [other_core(value) for value in mine]
    left_basis = call(
        "basis",
        functools.partial(basis_kernel, roles),
        shape(rows, vec),
        scratch_shapes=[
            pltpu.VMEM((order, 2 * order), jnp.float32),
            pltpu.VMEM((BLOCK, BLOCK), jnp.float32),
            pltpu.VMEM((BLOCK, BLOCK), jnp.float32),
            pltpu.VMEM((PANEL * PANEL, BLOCK), jnp.float32),
        ],
    )(*mine, *theirs, power)

    *shares, slab = call(
        "sides",
        sides_kernel,
        (shape(rows, cols),) * 4 + (shape(rows, order_size, dtype=jnp.bfloat16),),
        scratch_shapes=[pltpu.VMEM((cols, cols), jnp.bfloat16)],
    )(held)
    away = shares[2] + other_core(shares[0])
    left_sum = call("left", left_kernel, shape(rows, cols))(left_old, shares[3], other_core(shares[1]), weight)
    left_stat = call("last", last_kernel, shape(rows, cols))(left_sum, other_half(away), weight)
    owner_of = lambda shard: shard * rows // cols

    def from_owner(value, source, target):
        pairs = [
            tuple((owner_of(s) ^ bits) * shards + s for bits in (source, target)) for s in range(shards)
        ]
        return lax.ppermute(value, ("role", "shard"), pairs)

    crossed = from_owner(slab, 0, 2)
    right_stat = call("right", right_kernel, shape(rows, cols))(
        held, slab, from_owner(slab, 0, 1), crossed, from_owner(crossed, 2, 3), right_old, weight
    )
    return (left_stat, right_stat, left_basis)


def solution(mesh):
    return jax.shard_map(
        step,
        mesh=mesh,
        in_specs=(P("shard", "role"), P("shard", "role"), P("shard", "role"), P("shard", "role")),
        out_specs=(P("shard", "role"), P("shard", "role"), P("shard", "role")),
        check_vma=False,
    )
```
